32 devices in a mesh: gx: 4 (over z), gy: 8 (over y, x, core).
Axes of the slice: x: 2, y: 2, z: 4, core: 2. Of those that a mesh axis runs over, the one named last changes fastest.
Arguments:
- displacement: float32 [3, 128, 5, 1024], P(None, 'gx', None, 'gy'), may hold values from -5 to 5
- velocity: float32 [3, 128, 5, 1024], P(None, 'gx', None, 'gy'), may hold values from -4 to 4
- stiffness: float32 [128, 5, 1024], P('gx', None, 'gy'), may hold values from 0.5 to 2
- inverse_mass: float32 [128, 5, 1024], P('gx', None, 'gy'), may hold values from 0.5 to 2
- facing: int32 [128, 8, 8], P('gx', 'gy'), may hold values from 0 to 1023, as said below
Outputs:
- final_displacement: float32 [3, 128, 5, 1024], P(None, 'gx', None, 'gy')
- final_velocity: float32 [3, 128, 5, 1024], P(None, 'gx', None, 'gy')
The draws below stay inside these ranges and needn't reach their ends.
Inputs may be any that keep to these rules, and one draw needn't show every extreme that they name: facing[x, j, k] names block x' * 8 + j'. For each aligned run of 32 rows x and each j, the 256 entries name blocks with each pair (x' // 32, j') exactly 8 times; repeats are allowed.
All inputs are finite; a program needn't handle non-finite values.
Results may differ from the reference program's by a relative error of at most 0.0001.
Values sent between devices are 32-bit elements; how exact they have to be, the bound alone decides.
A program may use at most 64 MiB of HBM per device.

```python
import math
import jax
import jax.numpy as jnp
from jax import lax

CX = 32
CY = 128
NZ = 5
STEPS = 2
NX = 128
NY = 1024
GROUPS = 8
CAP = 8
DEVICES = 32


def draw_facing(key, part):
    requests = 8 * CX
    seed_list = jax.random.split(key, DEVICES)
    order_list = jax.vmap(lambda seed_one: jax.random.permutation(seed_one, requests))(seed_list)
    target_device = order_list // CAP
    target_row = jax.random.randint(jax.random.fold_in(key, 7), (DEVICES, requests), 0, CX)
    target_row = jnp.where(order_list == 0, 0, target_row)
    target_row = jnp.where(order_list == requests - 1, CX - 1, target_row)
    target_x = target_device // GROUPS * CX + target_row
    numbers = target_x * GROUPS + target_device % GROUPS
    shaped = numbers.reshape(DEVICES // GROUPS, GROUPS, CX, 8).transpose(0, 2, 1, 3)
    return shaped.reshape(NX, GROUPS, 8).astype(jnp.int32)


def block_levels(key, shape, cuts, low, largest):
    def one(axis_at, parts):
        steps = jax.random.uniform(jax.random.fold_in(jax.random.fold_in(key, 6), axis_at), (parts,), jnp.float32, low / len(cuts), largest / len(cuts))
        return jnp.repeat(jnp.exp(steps), shape[axis_at] // parts).reshape((-1,) + (1,) * (len(shape) - axis_at - 1))

    level = one(*cuts[0])
    for cut in cuts[1:]:
        level = level * one(*cut)
    return level


def scatter_about(key, extent, scale, limit, pieces=(), kind=jnp.bfloat16):
    factor_of = block_levels(key, extent, pieces, -0.22, 0.18) if pieces else 1.0
    drawn = jax.random.normal(key, extent, jnp.float32) * scale * factor_of
    return jnp.minimum(jnp.maximum(drawn, -limit), limit).astype(kind)


def setup_inputs(seed: int = 0) -> dict:
    key_of = jax.random.split(jax.random.key(seed), 6)
    displacement = scatter_about(key_of[0], (3, NX, NZ, NY), 1.0, 5.0, ((1, 4), (3, 8)), jnp.float32)
    velocity = scatter_about(key_of[1], (3, NX, NZ, NY), 0.5, 4.0, ((1, 4), (3, 8)), jnp.float32)
    stiffness = jnp.clip(jnp.exp(math.log(2.0) - 1.3862944 * jax.random.uniform(key_of[2], (NX, NZ, NY), jnp.float32) ** block_levels(key_of[2], (NX, NZ, NY), ((0, 4), (2, 8)), -0.2, 0.2)), 0.5, 2.0)
    inverse_mass = jnp.clip(jnp.exp(math.log(2.0) - 1.3862944 * jax.random.uniform(key_of[3], (NX, NZ, NY), jnp.float32) ** block_levels(key_of[3], (NX, NZ, NY), ((0, 4), (2, 8)), -0.2, 0.2)), 0.5, 2.0)
    facing = draw_facing(jax.random.fold_in(key_of[5], 71), 0)
    return dict(displacement=displacement, velocity=velocity, stiffness=stiffness, inverse_mass=inverse_mass, facing=facing)


time_step = 0.2
penalty = 4.0
damping = 1.0
kernel_width = 4.0
frame_extent = 4.0


def block_frame(block_size):
    place = (jnp.arange(block_size, dtype=jnp.float32) - (block_size - 1) / 2.0) * (frame_extent / block_size)
    zero_row = jnp.zeros((block_size,), jnp.float32)
    return jnp.stack([zero_row, place, zero_row], axis=0)


def pair_forces(own_block, facing_blocks):
    block_size = own_block.shape[-1]
    frame = block_frame(block_size)
    own_disp = own_block[:, :3] + frame
    own_vel = own_block[:, 3:]
    far_disp = facing_blocks[:, :, :3] + frame
    far_vel = facing_blocks[:, :, 3:]
    gaps = own_disp[:, None, :, :, None] - far_disp[:, :, :, None, :]
    spread = jnp.sum(gaps * gaps, axis=2)
    weights = jnp.exp(-spread / kernel_width)
    row_total = jnp.sum(weights, axis=3)
    col_total = jnp.sum(weights, axis=2)
    highest = lax.Precision.HIGHEST
    pulled_disp = jnp.einsum("gpij,gpcj->gpci", weights, far_disp, precision=highest)
    pulled_vel = jnp.einsum("gpij,gpcj->gpci", weights, far_vel, precision=highest)
    pushed_disp = jnp.einsum("gpij,gci->gpcj", weights, own_disp, precision=highest)
    pushed_vel = jnp.einsum("gpij,gci->gpcj", weights, own_vel, precision=highest)
    stiff_coef = penalty / (8.0 * block_size)
    damp_coef = damping / (8.0 * block_size)
    row_wide = row_total[:, :, None, :]
    col_wide = col_total[:, :, None, :]
    action = jnp.sum(stiff_coef * (own_disp[:, None] * row_wide - pulled_disp)
                     + damp_coef * (pulled_vel - own_vel[:, None] * row_wide), axis=1)
    reaction = -(stiff_coef * (pushed_disp - far_disp * col_wide)
                 + damp_coef * (far_vel * col_wide - pushed_vel))
    return action, reaction


def internal_force(padded_disp, padded_stiff, displacement):
    size_x, size_z, size_y = displacement.shape[1:]
    corner_sum = jnp.zeros((3, size_x + 1, size_z + 1, size_y + 1), jnp.float32)
    for shift_x in (0, 1):
        for shift_z in (0, 1):
            for shift_y in (0, 1):
                corner_sum = corner_sum + padded_disp[:, shift_x:shift_x + size_x + 1, shift_z:shift_z + size_z + 1, shift_y:shift_y + size_y + 1]
    mean_disp = corner_sum / 8.0
    element_stiff = padded_stiff[:size_x + 1, :size_z + 1, :size_y + 1]
    weighted = element_stiff[None] * mean_disp
    node_stiff = jnp.zeros((size_x, size_z, size_y), jnp.float32)
    node_pull = jnp.zeros((3, size_x, size_z, size_y), jnp.float32)
    for shift_x in (0, 1):
        for shift_z in (0, 1):
            for shift_y in (0, 1):
                node_stiff = node_stiff + element_stiff[shift_x:shift_x + size_x, shift_z:shift_z + size_z, shift_y:shift_y + size_y]
                node_pull = node_pull + weighted[:, shift_x:shift_x + size_x, shift_z:shift_z + size_z, shift_y:shift_y + size_y]
    return node_pull - displacement * node_stiff


def contact_force(displacement, velocity, facing):
    count_x, count_z, count_y = displacement.shape[1:]
    groups = count_y // CY
    blocks = count_x * groups
    surface = jnp.concatenate([displacement[:, :, count_z - 1, :], velocity[:, :, count_z - 1, :]], axis=0)
    blocked = surface.reshape(6, count_x, groups, CY).transpose(1, 2, 0, 3).reshape(blocks, 6, CY)
    targets = facing.reshape(blocks, 8)
    batch_size = 32

    def visit_group(accumulated, group_index):
        first_row = group_index * batch_size
        own_block = lax.dynamic_slice_in_dim(blocked, first_row, batch_size, 0)
        chosen = lax.dynamic_slice_in_dim(targets, first_row, batch_size, 0)
        facing_blocks = blocked[chosen]
        action, reaction = pair_forces(own_block, facing_blocks)
        current = lax.dynamic_slice_in_dim(accumulated, first_row, batch_size, 0)
        accumulated = lax.dynamic_update_slice_in_dim(accumulated, current + action, first_row, 0)
        accumulated = accumulated.at[chosen.reshape(-1)].add(reaction.reshape(batch_size * 8, 3, CY))
        return accumulated, None

    start_total = jnp.zeros((blocks, 3, CY), jnp.float32)
    accumulated, _ = lax.scan(visit_group, start_total, jnp.arange(blocks // batch_size, dtype=jnp.int32))
    return accumulated.reshape(count_x, groups, 3, CY).transpose(2, 0, 1, 3).reshape(3, count_x, count_y)


def reference(displacement, velocity, stiffness, inverse_mass, facing):
    count_x, count_z, count_y = stiffness.shape
    inside = ((jnp.arange(count_x, dtype=jnp.int32) < count_x - 1)[:, None, None]
              & (jnp.arange(count_z, dtype=jnp.int32) < count_z - 1)[None, :, None]
              & (jnp.arange(count_y, dtype=jnp.int32) < count_y - 1)[None, None, :])
    masked_stiff = jnp.where(inside, stiffness, 0.0)
    padded_stiff = jnp.pad(masked_stiff, 1)
    for repeat in range(STEPS):
        padded_disp = jnp.pad(displacement, ((0, 0), (1, 1), (1, 1), (1, 1)))
        internal = internal_force(padded_disp, padded_stiff, displacement)
        contact = contact_force(displacement, velocity, facing)
        total_force = internal.at[:, :, count_z - 1, :].add(contact)
        velocity = velocity + time_step * inverse_mass[None] * total_force
        displacement = displacement + time_step * velocity
    return displacement, velocity
```

```python
import functools
import math
import jax
import jax.numpy as jnp
from jax import lax
from jax.experimental import pallas as pl
from jax.experimental.pallas import tpu as pltpu
from jax.sharding import PartitionSpec as P

STEPS = 2

time_step = 0.2
penalty = 4.0
damping = 1.0
kernel_width = 4.0
frame_extent = 4.0

bf16 = jnp.bfloat16
f32 = jnp.float32
i32 = jnp.int32
MESH = pl.DeviceIdType.MESH
AHEAD = 2
PACK = 256


def split3(x):
    a = x.astype(bf16).astype(f32)
    r = x - a
    b = r.astype(bf16).astype(f32)
    return a, b, r - b


def table_kernel(count_gy, capacity, per_row, width_x, wanted_ref, out_ref):
    devices = out_ref.shape[0]
    requests = wanted_ref.shape[1]
    wanted = wanted_ref[...]
    wanted_x = wanted // count_gy
    device = wanted_x // width_x * count_gy + wanted % count_gy
    far = (wanted_x % width_x).astype(f32)
    own = (lax.broadcasted_iota(i32, (1, requests), 1) // per_row).astype(f32)
    mine = lax.broadcasted_iota(i32, (devices, requests), 0) == device
    mine_f = jnp.where(mine, 1.0, 0.0)
    upto = jnp.where(
        lax.broadcasted_iota(i32, (requests, requests), 0) <= lax.broadcasted_iota(i32, (requests, requests), 1), 1.0, 0.0
    ).astype(bf16)
    rank = jnp.dot(mine_f.astype(bf16), upto, preferred_element_type=f32)
    place = jnp.sum(mine_f * rank, axis=0, keepdims=True).astype(i32)
    at = jnp.where(lax.broadcasted_iota(i32, (128, requests), 0) + 1 == place, 1.0, 0.0).astype(bf16)
    dims = (((1,), (1,)), ((), ()))
    own_table = lax.dot_general((mine_f * own).astype(bf16), at, dims, preferred_element_type=f32)
    far_table = lax.dot_general((mine_f * far).astype(bf16), at, dims, preferred_element_type=f32)
    table = own_table.astype(i32) * PACK + far_table.astype(i32)
    for d in range(devices):
        out_ref[d] = table[d : d + 1]


def step_kernel(count_gx, count_gy, capacity, disp_ref, vel_ref, stiff_ref, mass_ref, table_v, table_s,
                u, v, kst, gath, edge, halo, far_table_v, far_table_s, flat, cur, own_a, own_b, acc, fint,
                zsend, psend, rsend, recv, hsend, hrecv, tsend, trecv, tlocal):
    depth, rows, width = stiff_ref.shape
    devices = count_gx * count_gy
    bits = count_gy.bit_length() - 1
    half = count_gy // 2
    fields = 4 * depth
    tall = -(-fields // 8) * 8
    gx = lax.axis_index("gx")
    gy = lax.axis_index("gy")
    me = gx * count_gy + gy
    order = [(k, m) for total in range(count_gx + half - 1) for m in range(half)
             for k in [total - m] if 0 <= k < count_gx]
    flips = [(1 - 2 * ((gy // (1 << k)) % 2)) * (1 << k) for k in range(bits)]
    side = gy % 2
    middle = list(range(1, bits))
    steps = [side * flips[b] + (1 - side) * flips[a] for a, b in zip(middle, middle[::-1])]
    steps.append(flips[0])

    def spot(j):
        k = jnp.int32(0)
        m = jnp.int32(0)
        for i, (a, b) in enumerate(order):
            if a:
                k = k + jnp.where(j == i, a, 0)
            if b:
                m = m + jnp.where(j == i, b, 0)
        return k, m

    def own_slot(k, m):
        column = gy
        for b in range(bits - 1):
            column = column + (m // (1 << b)) % 2 * steps[b]
        return lax.rem(gx + k, count_gx) * count_gy + column

    def partner_slot(k, m):
        column = gy + flips[0]
        for b in range(bits - 1):
            column = column + (m // (1 << b)) % 2 * steps[bits - 2 - b]
        return lax.rem(gx + k, count_gx) * count_gy + column

    def peer_of(p):
        return (p // count_gy, lax.rem(p, count_gy))

    barrier = pltpu.get_barrier_semaphore()

    @pl.loop(1, devices)
    def _(k):
        pl.semaphore_signal(barrier, inc=1, device_id=peer_of(lax.rem(me + k, devices)), device_id_type=MESH)

    lane = lax.broadcasted_iota(i32, (rows, width), 1)
    sub = lax.broadcasted_iota(i32, (rows, width), 0)
    lane_t = lax.broadcasted_iota(i32, (tall, width), 1)
    sub_t = lax.broadcasted_iota(i32, (tall, width), 0)
    lane1 = lax.broadcasted_iota(i32, (1, width), 1)
    row8 = lax.broadcasted_iota(i32, (8, width), 0)
    scale = math.sqrt(math.log2(math.e) / kernel_width)
    stiff_coef = penalty / (8.0 * width)
    damp_coef = damping / (8.0 * width)
    place = (lane.astype(f32) - (width - 1) / 2.0) * (frame_extent / width)
    inside = (sub + gx * rows < rows * count_gx - 1) & (lane + gy * width < width * count_gy - 1)

    u[...] = disp_ref[...]
    v[...] = vel_ref[...]
    for z in range(depth):
        kst[z] = jnp.where(inside, stiff_ref[z], 0.0) if z < depth - 1 else jnp.zeros((rows, width), f32)
    flat[pl.ds(4, rows, stride=8), :] = jnp.ones((rows, width), f32)

    around = [(dx, dy) for dx in (-1, 0, 1) for dy in (-1, 0, 1) if (dx, dy) != (0, 0)]
    base_of = {}
    size_of = {}
    start = 0
    for dx, dy in around:
        base_of[dx, dy] = start
        size_of[dx, dy] = rows if dx == 0 else (tall + 8 if dy == 0 else 8)
        start += size_of[dx, dy]

    def halo_copy(step, n):
        dx, dy = around[n]
        if dx == 0:
            first = tall
        elif dy == 0:
            first = 0 if dx < 0 else tall + rows - 8
        else:
            first = tall if dx < 0 else tall + rows - 8
        peer = (lax.rem(gx + dx + count_gx, count_gx), lax.rem(gy + dy + count_gy, count_gy))
        return pltpu.make_async_remote_copy(
            src_ref=edge.at[step, pl.ds(first, size_of[dx, dy])],
            dst_ref=halo.at[step, pl.ds(base_of[-dx, -dy], size_of[dx, dy])],
            send_sem=hsend.at[n],
            recv_sem=hrecv.at[step, n],
            device_id=peer,
            device_id_type=MESH,
        )

    def slot_copy(step, slot, peer, sem):
        return pltpu.make_async_remote_copy(
            src_ref=gath.at[step, slot],
            dst_ref=gath.at[step, slot],
            send_sem=sem,
            recv_sem=recv.at[step, slot],
            device_id=peer,
            device_id_type=MESH,
        )

    def table_copy(k):
        p = lax.rem(me + k, devices)
        return pltpu.make_async_remote_copy(
            src_ref=table_v.at[p],
            dst_ref=far_table_v.at[me],
            send_sem=tsend.at[k],
            recv_sem=trecv.at[me],
            device_id=peer_of(p),
            device_id_type=MESH,
        )

    def field(j):
        f, z = divmod(j, depth)
        return u[f, z] if f < 3 else kst[z]

    def slot_tiles(step, slot):
        n = None
        for c in range(3):
            s = gath[step, slot, c * rows : (c + 1) * rows]
            n = s * s if n is None else n + s * s
            flat[pl.ds(c, rows, stride=8), :] = s
            flat[pl.ds(5 + c, rows, stride=8), :] = gath[step, slot, (3 + c) * rows : (4 + c) * rows]
        flat[pl.ds(3, rows, stride=8), :] = -n
        cur[...] = flat[...].reshape(rows, 8, width)

    group_lane = lax.broadcasted_iota(i32, (width, 16 * capacity), 1) // 8
    one_lane = lax.broadcasted_iota(i32, (8, 8 * rows), 1)
    one_row = lax.broadcasted_iota(i32, (8, 8 * rows), 0) * rows
    blank = jnp.zeros((48, width), bf16)

    def slot_pairs(slot):
        pairs = []
        for p in range(capacity):
            t = table_s[slot, 0, p]
            pairs.append((lax.shift_right_logical(t, 8), t & (PACK - 1)))
            t = far_table_s[slot, 0, p]
            pairs.append((t & (PACK - 1), lax.shift_right_logical(t, 8)))
        fars = []
        pulls = []
        spots = []
        for r, b in pairs:
            x = cur[b]
            a, bq, c = split3(x)
            first = jnp.concatenate([a, bq], axis=0).astype(bf16)
            second = jnp.concatenate([c, a], axis=0).astype(bf16)
            fars.append(jnp.concatenate([first, first, second], axis=0))
            pulls.append(jnp.where(row8 >= 4, a, pltpu.roll(bq, 4, 0)))
            spots.append(jnp.where(one_lane == r + one_row, 1.0, 0.0))
        weights = []
        for h in range(capacity):
            far = jnp.concatenate([jnp.concatenate([fars[2 * h], blank], axis=1),
                                   jnp.concatenate([blank, fars[2 * h + 1]], axis=1)], axis=0)
            o = own_a[pairs[2 * h][0]] + own_b[pairs[2 * h + 1][0]]
            e = jnp.dot(o, far, preferred_element_type=f32)
            weights.append(jnp.exp2(e).astype(bf16))
        w = jnp.concatenate(weights, axis=1)
        pull = jnp.concatenate(pulls, axis=0).T.astype(bf16)
        rhs = jnp.concatenate([jnp.where(group_lane == p, pull, jnp.zeros_like(pull)) for p in range(2 * capacity)], axis=0)
        t = jnp.dot(w, rhs, preferred_element_type=f32)
        hi = t.astype(bf16)
        lo = (t - hi.astype(f32)).astype(bf16)
        s = jnp.concatenate(spots, axis=0).astype(bf16)
        return jnp.dot(hi, s, preferred_element_type=f32) + jnp.dot(lo, s, preferred_element_type=f32)

    def internal(step):
        def piece(dx, dy, first, size):
            return halo[step, pl.ds(base_of[dx, dy] + first, size), :]

        def down(x, last):
            return jnp.where(sub == rows - 1, last, pltpu.roll(x, rows - 1, 0))

        left = pltpu.roll(piece(0, -1, 0, rows), width // 2, 1)
        right = piece(0, 1, 0, rows)
        own_col = edge[step, pl.ds(tall, rows), :]
        top = piece(-1, 0, 8, tall)
        top_col = piece(-1, 0, 0, 8)[7:8]
        bottom = piece(1, 0, 0, tall)
        bottom_col = piece(1, 0, tall, 8)[0:1]
        top_left = pltpu.roll(piece(-1, -1, 0, 8), width // 2, 1)[7:8]
        top_right = piece(-1, 1, 0, 8)[7:8]
        bottom_left = pltpu.roll(piece(1, -1, 0, 8), width // 2, 1)[0:1]
        bottom_right = piece(1, 1, 0, 8)[0:1]
        own_row = edge[step, pl.ds(0, tall), :]

        right_sum = right + down(right, bottom_right)

        def column(sums, ks, lanes):
            zs = sums + pltpu.roll(sums, width - 1, 1)
            k = ks
            for f in range(3):
                k = jnp.where((lanes >= f * depth) & (lanes < (f + 1) * depth), pltpu.roll(ks, width - (3 - f) * depth, 1), k)
            g = jnp.where(lanes < 3 * depth, k * 0.125 * zs, jnp.where(lanes < fields, ks, 0.0))
            return g + pltpu.roll(g, 1, 1)

        col = left + own_col
        col_sum = col + down(col, bottom_left + bottom_col)
        col_part = column(col_sum, left, lane)
        corner8 = jnp.broadcast_to(top_left + top_col + col[0:1], (8, width))
        corner_k = jnp.broadcast_to(top_left, (8, width))
        corner = column(corner8, corner_k, lax.broadcasted_iota(i32, (8, width), 1))
        col_part = col_part + jnp.where(sub == 0, corner[0:1], pltpu.roll(col_part, 1, 0))

        row_sum = top + own_row
        end = jnp.broadcast_to(top_right + right[0:1], (tall, width))
        end = jnp.sum(jnp.where(lane_t == sub_t, end, 0.0), axis=1, keepdims=True)
        row_sum = row_sum + jnp.where(lane_t == width - 1, end, pltpu.roll(row_sum, width - 1, 1))
        row_sum = row_sum + pltpu.roll(row_sum, tall - 1, 0)
        k = top
        for f in range(3):
            k = jnp.where((sub_t >= f * depth) & (sub_t < (f + 1) * depth), pltpu.roll(top, tall - (3 - f) * depth, 0), k)
        g = jnp.where(sub_t < 3 * depth, k * 0.125 * row_sum, jnp.where(sub_t < fields, top, 0.0))
        g = g + pltpu.roll(g, 1, 0)
        row_part = g + jnp.where(lane_t == 0, 0.0, pltpu.roll(g, 1, 1))

        def spread(x, j):
            x = x + jnp.where(sub == 0, 0.0, pltpu.roll(x, 1, 0))
            x = x + jnp.where(lane == 0, 0.0, pltpu.roll(x, 1, 1))
            side_col = col_part if j == 0 else pltpu.roll(col_part, width - j, 1)
            x = x + jnp.where(lane == 0, side_col, 0.0)
            return x + jnp.where(sub == 0, row_part[j : j + 1], 0.0)

        ks = [kst[z] for z in range(depth - 1)]
        total_k = []
        for z in range(depth):
            x = ks[0] if z == 0 else (ks[z - 1] if z == depth - 1 else ks[z] + ks[z - 1])
            total_k.append(spread(x, 3 * depth + z))
        for f in range(3):
            flat = []
            for z in range(depth):
                j = f * depth + z
                x = u[f, z]
                x = x + down(x, bottom[j : j + 1])
                x = x + jnp.where(lane == width - 1, pltpu.roll(right_sum, width - 1 - j, 1), pltpu.roll(x, width - 1, 1))
                flat.append(x)
            g = [ks[z] * 0.125 * (flat[z] + flat[z + 1]) for z in range(depth - 1)]
            for z in range(depth):
                x = g[0] if z == 0 else (g[z - 1] if z == depth - 1 else g[z] + g[z - 1])
                fint[f, z] = spread(x, f * depth + z) - u[f, z] * total_k[z]

    def relay(step, j):
        k, m = spot(j)
        slot = own_slot(k, m)
        slot_copy(step, slot, peer_of(lax.rem(me + 1, devices)), psend.at[0]).wait_recv()
        for b in range(bits):
            @pl.when(m < (1 << b))
            def _(b=b):
                slot_copy(step, slot, (gx, gy + steps[b]), rsend.at[j, b]).start()

    @pl.loop(0, STEPS)
    def _(step):
        for c in range(3):
            p = u[c, depth - 1]
            if c == 1:
                p = p + place
            gath[step, me, c * rows : (c + 1) * rows] = scale * p
            gath[step, me, (3 + c) * rows : (4 + c) * rows] = stiff_coef * p - damp_coef * v[c, depth - 1]
        col = jnp.zeros((rows, width), f32)
        for j in range(fields):
            x = field(j)
            col = jnp.where(lane == j, x if j == 0 else pltpu.roll(x, j, 1), col)
            col = jnp.where(lane == width // 2 + j, pltpu.roll(x, width // 2 + 1 + j, 1), col)
            edge[step, j : j + 1] = x[0:1]
            edge[step, tall + rows + j : tall + rows + j + 1] = x[rows - 1 : rows]
        edge[step, tall : tall + rows] = col
        if tall > fields:
            edge[step, fields:tall] = jnp.zeros((tall - fields, width), f32)
            edge[step, tall + rows + fields :] = jnp.zeros((tall - fields, width), f32)

        @pl.when(step == 0)
        def _():
            pl.semaphore_wait(barrier, devices - 1)

        for k in range(1, count_gx):
            slot_copy(step, me, (lax.rem(gx + k, count_gx), gy), zsend.at[k]).start()
        for b in range(bits):
            slot_copy(step, me, (gx, gy + steps[b]), psend.at[b]).start()
        for n in range(len(around)):
            halo_copy(step, n).start()

        @pl.when(step == 0)
        def _():
            @pl.loop(1, devices)
            def _(k):
                table_copy(k).start()

        slot_tiles(step, me)

        @pl.loop(0, rows, unroll=4)
        def _(r):
            x = cur[r]
            norm = jnp.broadcast_to(x[3:4], x.shape)
            y = jnp.where(row8 < 3, 2.0 * x, jnp.where(row8 == 3, 1.0, jnp.where(row8 == 4, norm, 0.0)))
            a, b, c = split3(y)
            pack = jnp.concatenate([a, a, b, b, a, c], axis=0)
            zero = jnp.zeros_like(pack)
            own_a[r] = jnp.concatenate([pack, zero], axis=0).T.astype(bf16)
            own_b[r] = jnp.concatenate([zero, pack], axis=0).T.astype(bf16)

        @pl.loop(1, 1 + AHEAD)
        def _(j):
            relay(step, j)

        acc[...] = jnp.zeros_like(acc)

        for n in range(len(around)):
            halo_copy(step, n).wait_recv()
        internal(step)

        @pl.when(step == 0)
        def _():
            far_table_v[me] = table_v[me]

            @pl.loop(1, devices)
            def _(k):
                q = lax.rem(me + k, devices)
                pltpu.make_async_remote_copy(
                    src_ref=table_v.at[q], dst_ref=far_table_v.at[q], send_sem=tsend.at[k], recv_sem=trecv.at[q],
                    device_id=peer_of(q), device_id_type=MESH,
                ).wait_recv()
            keep = pltpu.make_async_copy(far_table_v, far_table_s, tlocal)
            keep.start()
            keep.wait()

        waves = len(order)

        @pl.loop(1, waves + 1)
        def _(j):
            @pl.when(j + AHEAD < waves)
            def _():
                relay(step, j + AHEAD)
            k, m = spot(j)
            slot = own_slot(k, m)
            slot_tiles(step, slot)
            one = slot_pairs(slot)
            k, m = spot(j - 1)
            slot = partner_slot(k, m)
            slot_copy(step, slot, peer_of(lax.rem(me + 1, devices)), psend.at[0]).wait_recv()
            slot_tiles(step, slot)
            acc[...] += one + slot_pairs(slot)

        total = acc[...]
        pieces = [total[:, i * width : (i + 1) * width].T for i in range(8 * rows // width)]
        total = pieces[0] if len(pieces) == 1 else jnp.concatenate(pieces, axis=0)
        count = total[4 * rows : 5 * rows]
        for c in range(3):
            q = gath[step, me, (3 + c) * rows : (4 + c) * rows]
            pulled = total[(5 + c) * rows : (6 + c) * rows] + total[(1 + c) * rows : (2 + c) * rows]
            fint[c, depth - 1] = fint[c, depth - 1] + q * count - pulled
        for z in range(depth):
            rate = time_step * mass_ref[z]
            for c in range(3):
                speed = v[c, z] + rate * fint[c, z]
                v[c, z] = speed
                u[c, z] = u[c, z] + time_step * speed

        for k in range(1, count_gx):
            slot_copy(step, me, (lax.rem(gx + k, count_gx), gy), zsend.at[k]).wait_send()
        for b in range(bits):
            slot_copy(step, me, (gx, gy + steps[b]), psend.at[b]).wait_send()
        for n in range(len(around)):
            halo_copy(step, n).wait_send()

        @pl.loop(1, waves)
        def _(j):
            k, m = spot(j)
            slot = own_slot(k, m)
            for b in range(bits):
                @pl.when(m < (1 << b))
                def _(b=b):
                    slot_copy(step, slot, (gx, gy + steps[b]), rsend.at[j, b]).wait_send()

        @pl.when(step == 0)
        def _():
            @pl.loop(1, devices)
            def _(k):
                table_copy(k).wait_send()


def local(displacement, velocity, stiffness, inverse_mass, facing):
    count_gx = lax.axis_size("gx")
    count_gy = lax.axis_size("gy")
    devices = count_gx * count_gy
    rows, depth, width = stiffness.shape
    per_row = facing.shape[2]
    requests = per_row * rows
    capacity = requests // devices
    bits = count_gy.bit_length() - 1
    waves = devices // 2
    fields = 4 * depth
    tall = -(-fields // 8) * 8
    vmem = pl.BlockSpec(memory_space=pltpu.VMEM)
    smem = pl.BlockSpec(memory_space=pltpu.SMEM)
    table = pl.pallas_call(
        functools.partial(table_kernel, count_gy, capacity, per_row, rows),
        out_shape=jax.ShapeDtypeStruct((devices, 1, 128), i32),
        in_specs=[vmem],
        out_specs=vmem,
        name="tables",
    )(facing.reshape(1, requests))
    whole = (3, depth, rows, width)
    dma = pltpu.SemaphoreType.DMA
    u, v = pl.pallas_call(
        functools.partial(step_kernel, count_gx, count_gy, capacity),
        out_shape=(jax.ShapeDtypeStruct(whole, f32), jax.ShapeDtypeStruct(whole, f32)),
        in_specs=[vmem] * 5 + [smem],
        out_specs=(vmem, vmem),
        scratch_shapes=[
            pltpu.VMEM((depth, rows, width), f32),
            pltpu.VMEM((STEPS, devices, 6 * rows, width), f32),
            pltpu.VMEM((STEPS, 2 * tall + rows, width), f32),
            pltpu.VMEM((STEPS, 2 * rows + 2 * (tall + 8) + 32, width), f32),
            pltpu.VMEM((devices, 1, 128), i32),
            pltpu.SMEM((devices, 1, 128), i32),
            pltpu.VMEM((8 * rows, width), f32),
            pltpu.VMEM((rows, 8, width), f32),
            pltpu.VMEM((rows, width, 96), bf16),
            pltpu.VMEM((rows, width, 96), bf16),
            pltpu.VMEM((width, 8 * rows), f32),
            pltpu.VMEM(whole, f32),
            dma((count_gx,)),
            dma((bits,)),
            dma((waves, bits)),
            dma((STEPS, devices)),
            dma((8,)),
            dma((STEPS, 8)),
            dma((devices,)),
            dma((devices,)),
            dma,
        ],
        compiler_params=pltpu.CompilerParams(collective_id=0, has_side_effects=True),
        name="steps",
    )(
        displacement.transpose(0, 2, 1, 3),
        velocity.transpose(0, 2, 1, 3),
        stiffness.transpose(1, 0, 2),
        inverse_mass.transpose(1, 0, 2),
        table,
        table,
    )
    return u.transpose(0, 2, 1, 3), v.transpose(0, 2, 1, 3)


def solution(mesh):
    in_specs = (
        P(None, "gx", None, "gy"),
        P(None, "gx", None, "gy"),
        P("gx", None, "gy"),
        P("gx", None, "gy"),
        P("gx", "gy", None),
    )
    out_specs = (P(None, "gx", None, "gy"), P(None, "gx", None, "gy"))
    return jax.shard_map(local, mesh=mesh, in_specs=in_specs, out_specs=out_specs, check_vma=False)
```

```python
import functools
import math
import jax
import jax.numpy as jnp
from jax import lax
from jax.experimental import pallas as pl
from jax.experimental.pallas import tpu as pltpu
from jax.sharding import PartitionSpec as P

STEPS = 2

time_step = 0.2
penalty = 4.0
damping = 1.0
kernel_width = 4.0
frame_extent = 4.0

bf16 = jnp.bfloat16
f32 = jnp.float32
i32 = jnp.int32
MESH = pl.DeviceIdType.MESH
AHEAD = 2
PACK = 256


def split3(x):
    a = x.astype(bf16).astype(f32)
    r = x - a
    b = r.astype(bf16).astype(f32)
    return a, b, r - b


def table_kernel(count_gy, capacity, per_row, width_x, wanted_ref, out_ref):
    devices = out_ref.shape[0]
    requests = wanted_ref.shape[1]
    wanted = wanted_ref[...]
    wanted_x = wanted // count_gy
    device = wanted_x // width_x * count_gy + wanted % count_gy
    far = (wanted_x % width_x).astype(f32)
    own = (lax.broadcasted_iota(i32, (1, requests), 1) // per_row).astype(f32)
    mine = lax.broadcasted_iota(i32, (devices, requests), 0) == device
    mine_f = jnp.where(mine, 1.0, 0.0)
    upto = jnp.where(
        lax.broadcasted_iota(i32, (requests, requests), 0) <= lax.broadcasted_iota(i32, (requests, requests), 1), 1.0, 0.0
    ).astype(bf16)
    rank = jnp.dot(mine_f.astype(bf16), upto, preferred_element_type=f32)
    place = jnp.sum(mine_f * rank, axis=0, keepdims=True).astype(i32)
    at = jnp.where(lax.broadcasted_iota(i32, (128, requests), 0) + 1 == place, 1.0, 0.0).astype(bf16)
    dims = (((1,), (1,)), ((), ()))
    own_table = lax.dot_general((mine_f * own).astype(bf16), at, dims, preferred_element_type=f32)
    far_table = lax.dot_general((mine_f * far).astype(bf16), at, dims, preferred_element_type=f32)
    table = own_table.astype(i32) * PACK + far_table.astype(i32)
    for d in range(devices):
        out_ref[d] = table[d : d + 1]


def step_kernel(count_gx, count_gy, capacity, disp_ref, vel_ref, stiff_ref, mass_ref, table_v, table_s,
                u, v, kst, gath, edge, halo, far_table_v, far_table_s, flat, cur, own_a, own_b, acc, fint,
                zsend, psend, rsend, recv, hsend, hrecv, tsend, trecv, tlocal):
    depth, rows, width = stiff_ref.shape
    devices = count_gx * count_gy
    bits = count_gy.bit_length() - 1
    half = count_gy // 2
    fields = 4 * depth
    tall = -(-fields // 8) * 8
    gx = lax.axis_index("gx")
    gy = lax.axis_index("gy")
    me = gx * count_gy + gy
    order = sorted(((k, m) for k in range(count_gx) for m in range(half)), key=lambda a: (a[0] + 1.6 * a[1], a[1]))
    flips = [(1 - 2 * ((gy // (1 << k)) % 2)) * (1 << k) for k in range(bits)]
    side = gy % 2
    middle = list(range(1, bits))
    steps = [side * flips[b] + (1 - side) * flips[a] for a, b in zip(middle, middle[::-1])]
    steps.append(flips[0])

    def spot(j):
        k = jnp.int32(0)
        m = jnp.int32(0)
        for i, (a, b) in enumerate(order):
            if a:
                k = k + jnp.where(j == i, a, 0)
            if b:
                m = m + jnp.where(j == i, b, 0)
        return k, m

    room = jnp.minimum(gx, count_gx - 1 - gx)
    toward = jnp.where(count_gx - 1 - gx > gx, 1, -1)

    def source(k):
        near = jnp.where(lax.rem(k, 2) == 1, lax.div(k + 1, 2), -lax.div(k, 2))
        return gx + jnp.where(k <= 2 * room, near, toward * (k - room))

    def own_slot(k, m):
        column = gy
        for b in range(bits - 1):
            column = column + (m // (1 << b)) % 2 * steps[b]
        return source(k) * count_gy + column

    def partner_slot(k, m):
        column = gy + flips[0]
        for b in range(bits - 1):
            column = column + (m // (1 << b)) % 2 * steps[bits - 2 - b]
        return source(k) * count_gy + column

    def peer_of(p):
        return (p // count_gy, lax.rem(p, count_gy))

    barrier = pltpu.get_barrier_semaphore()

    @pl.loop(1, devices)
    def _(k):
        pl.semaphore_signal(barrier, inc=1, device_id=peer_of(lax.rem(me + k, devices)), device_id_type=MESH)

    lane = lax.broadcasted_iota(i32, (rows, width), 1)
    sub = lax.broadcasted_iota(i32, (rows, width), 0)
    lane_t = lax.broadcasted_iota(i32, (tall, width), 1)
    sub_t = lax.broadcasted_iota(i32, (tall, width), 0)
    lane1 = lax.broadcasted_iota(i32, (1, width), 1)
    row8 = lax.broadcasted_iota(i32, (8, width), 0)
    scale = math.sqrt(math.log2(math.e) / kernel_width)
    stiff_coef = penalty / (8.0 * width)
    damp_coef = damping / (8.0 * width)
    place = (lane.astype(f32) - (width - 1) / 2.0) * (frame_extent / width)
    inside = (sub + gx * rows < rows * count_gx - 1) & (lane + gy * width < width * count_gy - 1)

    u[...] = disp_ref[...]
    v[...] = vel_ref[...]
    for z in range(depth):
        kst[z] = jnp.where(inside, stiff_ref[z], 0.0) if z < depth - 1 else jnp.zeros((rows, width), f32)
    for i in range(2):
        flat[i, pl.ds(4, rows, stride=8), :] = jnp.ones((rows, width), f32)

    around = [(dx, dy) for dx in (-1, 0, 1) for dy in (-1, 0, 1) if (dx, dy) != (0, 0)]
    base_of = {}
    size_of = {}
    start = 0
    for dx, dy in around:
        base_of[dx, dy] = start
        size_of[dx, dy] = rows if dx == 0 else (tall + 8 if dy == 0 else 8)
        start += size_of[dx, dy]

    def halo_copy(step, n):
        dx, dy = around[n]
        if dx == 0:
            first = tall
        elif dy == 0:
            first = 0 if dx < 0 else tall + rows - 8
        else:
            first = tall if dx < 0 else tall + rows - 8
        peer = (lax.rem(gx + dx + count_gx, count_gx), lax.rem(gy + dy + count_gy, count_gy))
        return pltpu.make_async_remote_copy(
            src_ref=edge.at[step, pl.ds(first, size_of[dx, dy])],
            dst_ref=halo.at[step, pl.ds(base_of[-dx, -dy], size_of[dx, dy])],
            send_sem=hsend.at[n],
            recv_sem=hrecv.at[step, n],
            device_id=peer,
            device_id_type=MESH,
        )

    def slot_copy(step, slot, peer, sem):
        return pltpu.make_async_remote_copy(
            src_ref=gath.at[step, slot],
            dst_ref=gath.at[step, slot],
            send_sem=sem,
            recv_sem=recv.at[step, slot],
            device_id=peer,
            device_id_type=MESH,
        )

    def table_copy(k):
        p = lax.rem(me + k, devices)
        return pltpu.make_async_remote_copy(
            src_ref=table_v.at[p],
            dst_ref=far_table_v.at[me],
            send_sem=tsend.at[k],
            recv_sem=trecv.at[me],
            device_id=peer_of(p),
            device_id_type=MESH,
        )

    def field(j):
        f, z = divmod(j, depth)
        return u[f, z] if f < 3 else kst[z]

    def slot_tiles(step, slot, i):
        n = None
        for c in range(3):
            s = gath[step, slot, c * rows : (c + 1) * rows]
            n = s * s if n is None else n + s * s
            flat[i, pl.ds(c, rows, stride=8), :] = s
            flat[i, pl.ds(5 + c, rows, stride=8), :] = gath[step, slot, (3 + c) * rows : (4 + c) * rows]
        flat[i, pl.ds(3, rows, stride=8), :] = -n
        cur[i] = flat[i].reshape(rows, 8, width)

    group_lane = lax.broadcasted_iota(i32, (width, 16 * capacity), 1) // 8
    one_lane = lax.broadcasted_iota(i32, (8, 8 * rows), 1)
    one_row = lax.broadcasted_iota(i32, (8, 8 * rows), 0) * rows
    blank = jnp.zeros((48, width), bf16)

    def slot_pairs(slot, i):
        pairs = []
        for p in range(capacity):
            t = table_s[slot, 0, p]
            pairs.append((lax.shift_right_logical(t, 8), t & (PACK - 1)))
            t = far_table_s[slot, 0, p]
            pairs.append((t & (PACK - 1), lax.shift_right_logical(t, 8)))
        fars = []
        pulls = []
        spots = []
        for r, b in pairs:
            x = cur[i, b]
            a, bq, c = split3(x)
            first = jnp.concatenate([a, bq], axis=0).astype(bf16)
            second = jnp.concatenate([c, a], axis=0).astype(bf16)
            fars.append(jnp.concatenate([first, first, second], axis=0))
            pulls.append(jnp.where(row8 >= 4, a, pltpu.roll(bq, 4, 0)))
            spots.append(jnp.where(one_lane == r + one_row, 1.0, 0.0))
        weights = []
        for h in range(capacity):
            far = jnp.concatenate([jnp.concatenate([fars[2 * h], blank], axis=1),
                                   jnp.concatenate([blank, fars[2 * h + 1]], axis=1)], axis=0)
            o = own_a[pairs[2 * h][0]] + own_b[pairs[2 * h + 1][0]]
            e = jnp.dot(o, far, preferred_element_type=f32)
            weights.append(jnp.exp2(e).astype(bf16))
        w = jnp.concatenate(weights, axis=1)
        pull = jnp.concatenate(pulls, axis=0).T.astype(bf16)
        rhs = jnp.concatenate([jnp.where(group_lane == p, pull, jnp.zeros_like(pull)) for p in range(2 * capacity)], axis=0)
        t = jnp.dot(w, rhs, preferred_element_type=f32)
        hi = t.astype(bf16)
        lo = (t - hi.astype(f32)).astype(bf16)
        s = jnp.concatenate(spots, axis=0).astype(bf16)
        return jnp.dot(hi, s, preferred_element_type=f32) + jnp.dot(lo, s, preferred_element_type=f32)

    def internal(step):
        def piece(dx, dy, first, size):
            return halo[step, pl.ds(base_of[dx, dy] + first, size), :]

        def down(x, last):
            return jnp.where(sub == rows - 1, last, pltpu.roll(x, rows - 1, 0))

        left = pltpu.roll(piece(0, -1, 0, rows), width // 2, 1)
        right = piece(0, 1, 0, rows)
        own_col = edge[step, pl.ds(tall, rows), :]
        top = piece(-1, 0, 8, tall)
        top_col = piece(-1, 0, 0, 8)[7:8]
        bottom = piece(1, 0, 0, tall)
        bottom_col = piece(1, 0, tall, 8)[0:1]
        top_left = pltpu.roll(piece(-1, -1, 0, 8), width // 2, 1)[7:8]
        top_right = piece(-1, 1, 0, 8)[7:8]
        bottom_left = pltpu.roll(piece(1, -1, 0, 8), width // 2, 1)[0:1]
        bottom_right = piece(1, 1, 0, 8)[0:1]
        own_row = edge[step, pl.ds(0, tall), :]

        right_sum = right + down(right, bottom_right)

        def column(sums, ks, lanes):
            zs = sums + pltpu.roll(sums, width - 1, 1)
            k = ks
            for f in range(3):
                k = jnp.where((lanes >= f * depth) & (lanes < (f + 1) * depth), pltpu.roll(ks, width - (3 - f) * depth, 1), k)
            g = jnp.where(lanes < 3 * depth, k * 0.125 * zs, jnp.where(lanes < fields, ks, 0.0))
            return g + pltpu.roll(g, 1, 1)

        col = left + own_col
        col_sum = col + down(col, bottom_left + bottom_col)
        col_part = column(col_sum, left, lane)
        corner8 = jnp.broadcast_to(top_left + top_col + col[0:1], (8, width))
        corner_k = jnp.broadcast_to(top_left, (8, width))
        corner = column(corner8, corner_k, lax.broadcasted_iota(i32, (8, width), 1))
        col_part = col_part + jnp.where(sub == 0, corner[0:1], pltpu.roll(col_part, 1, 0))

        row_sum = top + own_row
        end = jnp.broadcast_to(top_right + right[0:1], (tall, width))
        end = jnp.sum(jnp.where(lane_t == sub_t, end, 0.0), axis=1, keepdims=True)
        row_sum = row_sum + jnp.where(lane_t == width - 1, end, pltpu.roll(row_sum, width - 1, 1))
        row_sum = row_sum + pltpu.roll(row_sum, tall - 1, 0)
        k = top
        for f in range(3):
            k = jnp.where((sub_t >= f * depth) & (sub_t < (f + 1) * depth), pltpu.roll(top, tall - (3 - f) * depth, 0), k)
        g = jnp.where(sub_t < 3 * depth, k * 0.125 * row_sum, jnp.where(sub_t < fields, top, 0.0))
        g = g + pltpu.roll(g, 1, 0)
        row_part = g + jnp.where(lane_t == 0, 0.0, pltpu.roll(g, 1, 1))

        def spread(x, j):
            x = x + jnp.where(sub == 0, 0.0, pltpu.roll(x, 1, 0))
            x = x + jnp.where(lane == 0, 0.0, pltpu.roll(x, 1, 1))
            side_col = col_part if j == 0 else pltpu.roll(col_part, width - j, 1)
            x = x + jnp.where(lane == 0, side_col, 0.0)
            return x + jnp.where(sub == 0, row_part[j : j + 1], 0.0)

        ks = [kst[z] for z in range(depth - 1)]
        total_k = []
        for z in range(depth):
            x = ks[0] if z == 0 else (ks[z - 1] if z == depth - 1 else ks[z] + ks[z - 1])
            total_k.append(spread(x, 3 * depth + z))
        for f in range(3):
            flat = []
            for z in range(depth):
                j = f * depth + z
                x = u[f, z]
                x = x + down(x, bottom[j : j + 1])
                x = x + jnp.where(lane == width - 1, pltpu.roll(right_sum, width - 1 - j, 1), pltpu.roll(x, width - 1, 1))
                flat.append(x)
            g = [ks[z] * 0.125 * (flat[z] + flat[z + 1]) for z in range(depth - 1)]
            for z in range(depth):
                x = g[0] if z == 0 else (g[z - 1] if z == depth - 1 else g[z] + g[z - 1])
                fint[f, z] = spread(x, f * depth + z) - u[f, z] * total_k[z]

    def relay(step, j):
        k, m = spot(j)
        slot = own_slot(k, m)
        slot_copy(step, slot, peer_of(lax.rem(me + 1, devices)), psend.at[0]).wait_recv()
        for b in range(bits):
            @pl.when(m < (1 << b))
            def _(b=b):
                slot_copy(step, slot, (gx, gy + steps[b]), rsend.at[j, b]).start()

    @pl.loop(0, STEPS)
    def _(step):
        for c in range(3):
            p = u[c, depth - 1]
            if c == 1:
                p = p + place
            gath[step, me, c * rows : (c + 1) * rows] = scale * p
            gath[step, me, (3 + c) * rows : (4 + c) * rows] = stiff_coef * p - damp_coef * v[c, depth - 1]
        col = jnp.zeros((rows, width), f32)
        for j in range(fields):
            x = field(j)
            col = jnp.where(lane == j, x if j == 0 else pltpu.roll(x, j, 1), col)
            col = jnp.where(lane == width // 2 + j, pltpu.roll(x, width // 2 + 1 + j, 1), col)
            edge[step, j : j + 1] = x[0:1]
            edge[step, tall + rows + j : tall + rows + j + 1] = x[rows - 1 : rows]
        edge[step, tall : tall + rows] = col
        if tall > fields:
            edge[step, fields:tall] = jnp.zeros((tall - fields, width), f32)
            edge[step, tall + rows + fields :] = jnp.zeros((tall - fields, width), f32)

        @pl.when(step == 0)
        def _():
            pl.semaphore_wait(barrier, devices - 1)

        for k in range(1, count_gx):
            slot_copy(step, me, (source(jnp.int32(k)), gy), zsend.at[k]).start()
        for b in range(bits):
            slot_copy(step, me, (gx, gy + steps[b]), psend.at[b]).start()
        for n in range(len(around)):
            halo_copy(step, n).start()

        @pl.when(step == 0)
        def _():
            @pl.loop(1, devices)
            def _(k):
                table_copy(k).start()

        slot_tiles(step, me, 0)

        def prepare(r):
            x = cur[0, r]
            norm = jnp.broadcast_to(x[3:4], x.shape)
            y = jnp.where(row8 < 3, 2.0 * x, jnp.where(row8 == 3, 1.0, jnp.where(row8 == 4, norm, 0.0)))
            a, b, c = split3(y)
            pack = jnp.concatenate([a, a, b, b, a, c], axis=0)
            zero = jnp.zeros_like(pack)
            own_a[r] = jnp.concatenate([pack, zero], axis=0).T.astype(bf16)
            own_b[r] = jnp.concatenate([zero, pack], axis=0).T.astype(bf16)

        pl.loop(0, rows // 2, unroll=4)(prepare)

        @pl.loop(1, 1 + AHEAD)
        def _(j):
            relay(step, j)

        pl.loop(rows // 2, rows, unroll=4)(prepare)

        acc[...] = jnp.zeros_like(acc)

        for n in range(len(around)):
            halo_copy(step, n).wait_recv()
        internal(step)

        @pl.when(step == 0)
        def _():
            far_table_v[me] = table_v[me]

            @pl.loop(1, devices)
            def _(k):
                q = lax.rem(me + k, devices)
                pltpu.make_async_remote_copy(
                    src_ref=table_v.at[q], dst_ref=far_table_v.at[q], send_sem=tsend.at[k], recv_sem=trecv.at[q],
                    device_id=peer_of(q), device_id_type=MESH,
                ).wait_recv()
            keep = pltpu.make_async_copy(far_table_v, far_table_s, tlocal)
            keep.start()
            keep.wait()

        waves = len(order)

        @pl.loop(0, waves)
        def _(j):
            @pl.when((j > 0) & (j + AHEAD < waves))
            def _():
                relay(step, j + AHEAD)
            k, m = spot(j)
            mine = own_slot(k, m)
            other = partner_slot(k, m)
            slot_copy(step, other, peer_of(lax.rem(me + 1, devices)), psend.at[0]).wait_recv()
            slot_tiles(step, mine, 0)
            slot_tiles(step, other, 1)
            acc[...] += slot_pairs(mine, 0) + slot_pairs(other, 1)

        total = acc[...]
        pieces = [total[:, i * width : (i + 1) * width].T for i in range(8 * rows // width)]
        total = pieces[0] if len(pieces) == 1 else jnp.concatenate(pieces, axis=0)
        count = total[4 * rows : 5 * rows]
        for c in range(3):
            q = gath[step, me, (3 + c) * rows : (4 + c) * rows]
            pulled = total[(5 + c) * rows : (6 + c) * rows] + total[(1 + c) * rows : (2 + c) * rows]
            fint[c, depth - 1] = fint[c, depth - 1] + q * count - pulled
        for z in range(depth):
            rate = time_step * mass_ref[z]
            for c in range(3):
                speed = v[c, z] + rate * fint[c, z]
                v[c, z] = speed
                u[c, z] = u[c, z] + time_step * speed

        for k in range(1, count_gx):
            slot_copy(step, me, (source(jnp.int32(k)), gy), zsend.at[k]).wait_send()
        for b in range(bits):
            slot_copy(step, me, (gx, gy + steps[b]), psend.at[b]).wait_send()
        for n in range(len(around)):
            halo_copy(step, n).wait_send()

        @pl.loop(1, waves)
        def _(j):
            k, m = spot(j)
            slot = own_slot(k, m)
            for b in range(bits):
                @pl.when(m < (1 << b))
                def _(b=b):
                    slot_copy(step, slot, (gx, gy + steps[b]), rsend.at[j, b]).wait_send()

        @pl.when(step == 0)
        def _():
            @pl.loop(1, devices)
            def _(k):
                table_copy(k).wait_send()


def local(displacement, velocity, stiffness, inverse_mass, facing):
    count_gx = lax.axis_size("gx")
    count_gy = lax.axis_size("gy")
    devices = count_gx * count_gy
    rows, depth, width = stiffness.shape
    per_row = facing.shape[2]
    requests = per_row * rows
    capacity = requests // devices
    bits = count_gy.bit_length() - 1
    waves = devices // 2
    fields = 4 * depth
    tall = -(-fields // 8) * 8
    vmem = pl.BlockSpec(memory_space=pltpu.VMEM)
    smem = pl.BlockSpec(memory_space=pltpu.SMEM)
    table = pl.pallas_call(
        functools.partial(table_kernel, count_gy, capacity, per_row, rows),
        out_shape=jax.ShapeDtypeStruct((devices, 1, 128), i32),
        in_specs=[vmem],
        out_specs=vmem,
        name="tables",
    )(facing.reshape(1, requests))
    whole = (3, depth, rows, width)
    dma = pltpu.SemaphoreType.DMA
    u, v = pl.pallas_call(
        functools.partial(step_kernel, count_gx, count_gy, capacity),
        out_shape=(jax.ShapeDtypeStruct(whole, f32), jax.ShapeDtypeStruct(whole, f32)),
        in_specs=[vmem] * 5 + [smem],
        out_specs=(vmem, vmem),
        scratch_shapes=[
            pltpu.VMEM((depth, rows, width), f32),
            pltpu.VMEM((STEPS, devices, 6 * rows, width), f32),
            pltpu.VMEM((STEPS, 2 * tall + rows, width), f32),
            pltpu.VMEM((STEPS, 2 * rows + 2 * (tall + 8) + 32, width), f32),
            pltpu.VMEM((devices, 1, 128), i32),
            pltpu.SMEM((devices, 1, 128), i32),
            pltpu.VMEM((2, 8 * rows, width), f32),
            pltpu.VMEM((2, rows, 8, width), f32),
            pltpu.VMEM((rows, width, 96), bf16),
            pltpu.VMEM((rows, width, 96), bf16),
            pltpu.VMEM((width, 8 * rows), f32),
            pltpu.VMEM(whole, f32),
            dma((count_gx,)),
            dma((bits,)),
            dma((waves, bits)),
            dma((STEPS, devices)),
            dma((8,)),
            dma((STEPS, 8)),
            dma((devices,)),
            dma((devices,)),
            dma,
        ],
        compiler_params=pltpu.CompilerParams(collective_id=0, has_side_effects=True),
        name="steps",
    )(
        displacement.transpose(0, 2, 1, 3),
        velocity.transpose(0, 2, 1, 3),
        stiffness.transpose(1, 0, 2),
        inverse_mass.transpose(1, 0, 2),
        table,
        table,
    )
    return u.transpose(0, 2, 1, 3), v.transpose(0, 2, 1, 3)


def solution(mesh):
    in_specs = (
        P(None, "gx", None, "gy"),
        P(None, "gx", None, "gy"),
        P("gx", None, "gy"),
        P("gx", None, "gy"),
        P("gx", "gy", None),
    )
    out_specs = (P(None, "gx", None, "gy"), P(None, "gx", None, "gy"))
    return jax.shard_map(local, mesh=mesh, in_specs=in_specs, out_specs=out_specs, check_vma=False)
```
